32 devices in a mesh: groups: 2 (over x), paths: 2 (over core), feats: 8 (over z, y).
Axes of the slice: x: 2, y: 2, z: 4, core: 2. Of those that a mesh axis runs over, the one named last changes fastest.
Arguments:
- factors: int32 [4096, 128], P(('groups', 'paths')), parts along dimension 0, may hold values from -8 to 8
- frequency: int32 [128, 65536], P(None, 'feats'), may hold values from -48 to 48
- phases: int32 [65536], P('feats'), may hold values from 0 to 1023
- amplitude: float32 [65536], P('feats'), as said below
- targets: float32 [32, 4096], P(None, ('groups', 'paths')), parts along dimension 1, may hold values from -6 to 6
- coeffs_init: float32 [32, 131072], P(None, ('groups', 'feats')), parts along dimension 1, may hold values from -6 to 6
Outputs:
- coeffs: float32 [32, 131072], P(None, ('groups', 'feats')), parts along dimension 1
- predicted: float32 [32, 4096], P(None, ('groups', 'paths')), parts along dimension 1
The draws below stay inside these ranges and needn't reach their ends.
There are 2 independent parts, one for each index of `groups`. The reference program is written for one: setup_inputs(seed, part) draws one part's arguments, and reference() takes and returns one part's arrays. A program takes and returns all parts, laid end to end along the dimension named above; an argument that names none is the same for every part. Nothing has to cross between parts.
Inputs may be any that keep to these rules, and one draw needn't show every extreme that they name: `amplitude`: positive feature weights.
All inputs are finite; a program needn't handle non-finite values.
Results may differ from the reference program's by a relative error of at most 0.00026.
Values sent between devices are 32-bit elements; how exact they have to be, the bound alone decides.
A program may use at most 128 MiB of HBM per device.

```python
import math
import jax
import jax.numpy as jnp
from jax import lax

F = 65536
K = 128
V = 32
ITERS = 3
PATHS = 2048


def draw_amplitude(key, part):
    index = jnp.arange(F, dtype=jnp.float32)
    rising = jnp.exp(jnp.log(3.0) * index / F)
    spread = jnp.exp(jax.random.uniform(key, (F,), jnp.float32, minval=-1.2, maxval=1.2))
    return (spread * rising * jnp.sqrt(1.0 / F)).astype(jnp.float32)


def place_ends(array, key, smallest, top_value):
    longest = array.shape.index(max(array.shape))
    spots = []
    for shift in (0, 1):
        where = [jax.random.randint(jax.random.fold_in(key, axis), (), 0, length) for axis, length in enumerate(array.shape)]
        where[longest] = (where[longest] + shift) % array.shape[longest]
        spots.append(tuple(where))
    return array.at[spots[0]].set(smallest).at[spots[1]].set(top_value)


def block_scale(own_key, shape, cuts, low, high):
    loudness, own = 1.0, jax.random.fold_in(own_key, 6)
    for position, shards_of in cuts:
        steps = jnp.exp(jax.random.uniform(jax.random.fold_in(own, position), (shards_of,), jnp.float32, low / len(cuts), high / len(cuts)))
        loudness = loudness * jnp.repeat(steps, shape[position] // shards_of).reshape([-1 if axis == position else 1 for axis in range(len(shape))])
    return loudness


def bell_draw(own_key, dims, scale, bound, pieces=(), held_as=jnp.bfloat16):
    level = block_scale(own_key, dims, pieces, -0.22, 0.18) if pieces else 1.0
    values = jax.random.normal(own_key, dims, jnp.float32) * scale * level
    return jnp.minimum(jnp.maximum(values, -bound), bound).astype(held_as)


def setup_inputs(seed: int = 0, part: int = 0) -> dict:
    streams_of = jax.random.split(jax.random.key(seed), 7)
    part_keys = jax.random.split(jax.random.fold_in(streams_of[6], part), 7)
    factors = place_ends(jax.random.randint(part_keys[0], (PATHS, K), -8, 9), jax.random.fold_in(part_keys[0], 1), -8, 8).astype(jnp.int32)
    frequency = place_ends(jax.random.randint(streams_of[1], (K, F), 0 - 6144 // K, 6144 // K + 1), jax.random.fold_in(streams_of[1], 1), 0 - 6144 // K, (6144 // K + 1) - 1).astype(jnp.int32)
    phases = place_ends(jax.random.randint(streams_of[2], (F,), 0, 1024), jax.random.fold_in(streams_of[2], 1), 0, 1023).astype(jnp.int32)
    amplitude = draw_amplitude(jax.random.fold_in(streams_of[6], 71), part)
    targets = bell_draw(part_keys[4], (V, PATHS), 1.0, 6.0, ((1, 2),), jnp.float32)
    coeffs_init = bell_draw(part_keys[5], (V, F), 1.0, 6.0, ((1, 8),), jnp.float32)
    return {"factors": factors, "frequency": frequency, "phases": phases, "amplitude": amplitude, "targets": targets, "coeffs_init": coeffs_init}


huber_cap = 1.0
step_rate = 0.2
momentum = 0.9
epsilon = 1e-06

def build(factor_vals, freq_block, phase_block, amp_block):
    summed = jnp.dot(factor_vals, freq_block, precision=lax.Precision.HIGHEST, preferred_element_type=jnp.float32)
    return amp_block * jnp.cos(summed * 0.0025 + phase_block * (2.0 * math.pi / 1024.0))

def reference(factors, frequency, phases, amplitude, targets, coeffs_init):
    block_cols = min(F, 2048)
    nblocks = F // block_cols
    total_paths = targets.shape[1]
    factor_vals = factors.astype(jnp.float32)
    freq_blocks = jnp.transpose(frequency.astype(jnp.float32).reshape(K, nblocks, block_cols), (1, 0, 2))
    phase_blocks = phases.astype(jnp.float32).reshape(nblocks, block_cols)
    amp_blocks = amplitude.reshape(nblocks, block_cols)

    def feature_block(index):
        return build(factor_vals, freq_blocks[index], phase_blocks[index], amp_blocks[index])

    def predict(coeffs):
        coeff_blocks = jnp.transpose(coeffs.reshape(V, nblocks, block_cols), (1, 0, 2))

        def step(total, index):
            block = feature_block(index)
            part = lax.dot_general(coeff_blocks[index], block, (((1,), (1,)), ((), ())), precision=lax.Precision.HIGHEST, preferred_element_type=jnp.float32)
            return (total + part, None)
        total, _ = lax.scan(step, jnp.zeros((V, total_paths), jnp.float32), jnp.arange(nblocks, dtype=jnp.int32))
        return total
    coeffs = coeffs_init
    velocity = jnp.zeros_like(coeffs_init)
    predicted = predict(coeffs)
    for turn in range(ITERS):
        clipped = jnp.clip(predicted - targets, -huber_cap, huber_cap)

        def grad_step(carry, index):
            block = feature_block(index)
            return (carry, jnp.dot(clipped, block, precision=lax.Precision.HIGHEST, preferred_element_type=jnp.float32))
        _, grad_blocks = lax.scan(grad_step, jnp.float32(0.0), jnp.arange(nblocks, dtype=jnp.int32))
        gradient = jnp.transpose(grad_blocks, (1, 0, 2)).reshape(V, F)
        scale = jnp.sqrt(jnp.mean(gradient * gradient) + epsilon)
        velocity = momentum * velocity + gradient / scale
        coeffs = coeffs - step_rate * velocity
        predicted = predict(coeffs)
    return (coeffs, predicted)
```

```python
import functools
import math

import jax
import jax.numpy as jnp
import numpy as np
from jax import lax
from jax.experimental import pallas as pl
from jax.experimental.pallas import tpu as pltpu
from jax.sharding import PartitionSpec as P

huber_cap = 1.0
step_rate = 0.2
momentum = 0.9
epsilon = 1e-06
ITERS = 3
BF = jnp.bfloat16
F32 = jnp.float32


def cosine_fit(degree):
    n = 64
    nodes = np.cos((np.arange(n) + 0.5) * np.pi / n)
    u = (nodes + 1.0) / 8.0
    cheb = np.polynomial.chebyshev.Chebyshev.fit(u, np.cos(2 * np.pi * np.sqrt(u)), degree, domain=[0.0, 0.25])
    return [float(c) for c in cheb.convert(kind=np.polynomial.Polynomial).coef]


COEFS = cosine_fit(5)
TURN = 0.0025 / (2.0 * math.pi)
MAGIC = 12582912.0


def cos_turns(t):
    k = (t + MAGIC) - MAGIC
    r = t - k
    u = r * r
    acc = u * COEFS[-1] + COEFS[-2]
    for c in COEFS[-3::-1]:
        acc = acc * u + c
    return acc


def split(x):
    hi = x.astype(BF)
    lo = (x - hi.astype(F32)).astype(BF)
    return hi, lo


def stacked(x):
    hi, lo = split(x)
    return jnp.concatenate([hi, lo], axis=0)


NT = (((1,), (1,)), ((), ()))


def build_kernel(half_ref, fac_ref, freq_ref, phase_ref, amp_ref, coef_ref, hi_ref, lo_ref, pred_ref, *, rows):
    @pl.when(pl.program_id(0) == 0)
    def _():
        pred_ref[...] = jnp.zeros_like(pred_ref)

    freq = freq_ref[...].astype(F32).astype(BF)
    phase = phase_ref[...].astype(F32) * (1.0 / 1024.0)
    chunks = fac_ref.shape[0] // rows

    def step(i, carry):
        at = pl.ds(pl.multiple_of(i * rows, rows), rows)
        summed = jnp.dot(fac_ref[at, :], freq, preferred_element_type=F32)
        c = cos_turns(summed * TURN + phase)
        hi, lo = split(c)
        hi_ref[at, :] = hi
        lo_ref[at, :] = lo
        return carry

    lax.fori_loop(0, chunks, step, 0, unroll=2)
    v = coef_ref.shape[0]
    x = stacked(coef_ref[...] * amp_ref[...])
    out = lax.dot_general(x, hi_ref[...], NT, preferred_element_type=F32)
    out = out + lax.dot_general(x, lo_ref[...], NT, preferred_element_type=F32)
    pred_ref[...] += out[:v] + out[v:]


def build(half, factors, frequency, phases, amplitude, coeffs, tile):
    paths, k = factors.shape
    v, whole = coeffs.shape
    mine = whole // 2
    nb = mine // tile
    at = lambda i, h: (0, h[0] * nb + i)
    return pl.pallas_call(
        functools.partial(build_kernel, rows=128),
        grid_spec=pltpu.PrefetchScalarGridSpec(
            num_scalar_prefetch=1,
            grid=(nb,),
            in_specs=[
                pl.BlockSpec((paths, k), lambda i, h: (0, 0)),
                pl.BlockSpec((k, tile), at),
                pl.BlockSpec((1, tile), at),
                pl.BlockSpec((1, tile), at),
                pl.BlockSpec((v, tile), at),
            ],
            out_specs=[
                pl.BlockSpec((paths, tile), lambda i, h: (0, i)),
                pl.BlockSpec((paths, tile), lambda i, h: (0, i)),
                pl.BlockSpec((v, paths), lambda i, h: (0, 0)),
            ],
        ),
        out_shape=[
            jax.ShapeDtypeStruct((paths, mine), BF),
            jax.ShapeDtypeStruct((paths, mine), BF),
            jax.ShapeDtypeStruct((v, paths), F32),
        ],
        name="build",
    )(half, factors, frequency, phases, amplitude, coeffs)


def turn_kernel(half_ref, clip_ref, amp_ref, hi_ref, lo_ref, grad_ref, push_ref, sq_ref, clip_pair):
    @pl.when(pl.program_id(0) == 0)
    def _():
        push_ref[...] = jnp.zeros_like(push_ref)
        sq_ref[...] = jnp.zeros_like(sq_ref)
        clip_pair[...] = stacked(clip_ref[...])

    v = grad_ref.shape[0]
    x = clip_pair[...]
    g = jnp.dot(x, hi_ref[...], preferred_element_type=F32)
    g = g + jnp.dot(x, lo_ref[...], preferred_element_type=F32)
    amp = amp_ref[...]
    grad = (g[:v] + g[v:]) * amp
    grad_ref[...] = grad
    square = grad * grad
    fold = sum(square[r : r + 8] for r in range(0, v, 8))
    sq_ref[...] += sum(fold[:, c : c + 128] for c in range(0, fold.shape[1], 128))
    y = stacked(grad * amp)
    out = lax.dot_general(y, hi_ref[...], NT, preferred_element_type=F32)
    out = out + lax.dot_general(y, lo_ref[...], NT, preferred_element_type=F32)
    push_ref[...] += out[:v] + out[v:]


def turn(half, clipped, amplitude, hi, lo, tile):
    v, paths = clipped.shape
    mine = hi.shape[1]
    nb = mine // tile
    return pl.pallas_call(
        turn_kernel,
        grid_spec=pltpu.PrefetchScalarGridSpec(
            num_scalar_prefetch=1,
            grid=(nb,),
            in_specs=[
                pl.BlockSpec((v, paths), lambda i, h: (0, 0)),
                pl.BlockSpec((1, tile), lambda i, h: (0, h[0] * nb + i)),
                pl.BlockSpec((paths, tile), lambda i, h: (0, i)),
                pl.BlockSpec((paths, tile), lambda i, h: (0, i)),
            ],
            out_specs=[
                pl.BlockSpec((v, tile), lambda i, h: (0, i)),
                pl.BlockSpec((v, paths), lambda i, h: (0, 0)),
                pl.BlockSpec((8, 128), lambda i, h: (0, 0)),
            ],
            scratch_shapes=[pltpu.VMEM((2 * v, paths), BF)],
        ),
        out_shape=[
            jax.ShapeDtypeStruct((v, mine), F32),
            jax.ShapeDtypeStruct((v, paths), F32),
            jax.ShapeDtypeStruct((8, 128), F32),
        ],
        name="turn",
    )(half, clipped, amplitude, hi, lo)


MESH = pl.DeviceIdType.MESH


def sum_kernel(x_ref, sq_ref, out_ref, sqout_ref, from_pair, chip, pieces, result, sq_pair, sq_mine, sq_all, total,
               pair_send, pair_recv, rs_send, rs_recv, ag_send, ag_recv, back_send, back_recv, sqp_sem, sqs_send, sqs_recv,
               *, n, rows, width, per_row):
    v, half_cols = chip.shape
    core = lax.axis_index("paths")
    me = lax.axis_index("feats")
    other = 1 - core

    barrier = pltpu.get_barrier_semaphore()
    pl.semaphore_signal(barrier, inc=1, device_id={"paths": other}, device_id_type=MESH)
    for d in range(1, n):
        pl.semaphore_signal(barrier, inc=1, device_id={"feats": lax.rem(me + d, n)}, device_id_type=MESH)
    pl.semaphore_wait(barrier, n)

    def spot(j, base):
        r = pl.ds(pl.multiple_of((j // per_row) * rows, rows), rows)
        c = pl.ds(pl.multiple_of(base + lax.rem(j, per_row) * width, width), width)
        return r, c

    def to_pair(src, dst, ss, rs):
        return pltpu.make_async_remote_copy(src, dst, ss, rs, device_id={"paths": other}, device_id_type=MESH)

    def to_chip(src, dst, ss, rs, j):
        return pltpu.make_async_remote_copy(src, dst, ss, rs, device_id={"feats": j}, device_id_type=MESH)

    zero = 0
    sq_copy = to_pair(sq_ref, sq_pair, sqp_sem.at[0], sqp_sem.at[1])
    sq_copy.start()
    pair_copies = []
    for d in range(1, n + 1):
        j = lax.rem(me + d, n)
        r, c = spot(j, other * half_cols)
        r2, c2 = spot(j, zero)
        pair_copies.append(to_pair(x_ref.at[r, c], from_pair.at[r2, c2], pair_send.at[d - 1], pair_recv.at[d - 1]))
        pair_copies[-1].start()

    sq_copy.wait()
    sq_mine[...] = sq_ref[...] + sq_pair[...]
    sq_all[me] = sq_mine[...]
    rs_copies, sq_copies = [], []
    for d in range(1, n + 1):
        j = lax.rem(me + d, n)
        pair_copies[d - 1].wait_recv()
        r, c = spot(j, core * half_cols)
        r2, c2 = spot(j, zero)
        chip[r2, c2] = x_ref[r, c] + from_pair[r2, c2]
        if d < n:
            rs_copies.append(to_chip(chip.at[r2, c2], pieces.at[d - 1], rs_send.at[d - 1], rs_recv.at[d - 1], j))
            rs_copies[-1].start()
    for d in range(1, n):
        j = lax.rem(me + d, n)
        sq_copies.append(to_chip(sq_mine, sq_all.at[me], sqs_send.at[d - 1], sqs_recv.at[d - 1], j))
        sq_copies[-1].start()

    mr, mc = spot(me, zero)
    acc = chip[mr, mc]
    for d in range(1, n):
        rs_copies[d - 1].wait_recv()
        acc = acc + pieces[d - 1]
    total[...] = acc

    br, bc = spot(me, core * half_cols)
    ag_copies, back_copies = [], []
    for d in range(1, n):
        j = lax.rem(me + d, n)
        ag_copies.append(to_chip(total, result.at[br, bc], ag_send.at[d - 1], ag_recv.at[d - 1], j))
        ag_copies[-1].start()
    back_copies.append(to_pair(total, result.at[br, bc], back_send.at[0], back_recv.at[0]))
    back_copies[0].start()
    result[br, bc] = acc
    for d in range(1, n):
        ag_copies[d - 1].wait_recv()
        source = lax.rem(me + n - d, n)
        r, c = spot(source, core * half_cols)
        back_copies.append(to_pair(result.at[r, c], result.at[r, c], back_send.at[d], back_recv.at[d]))
        back_copies[-1].start()
    for copy in sq_copies:
        copy.wait()
    sqout_ref[...] = jnp.broadcast_to(jnp.sum(jnp.sum(sq_all[...], axis=0), keepdims=True), sqout_ref.shape)
    for copy in pair_copies:
        copy.wait_send()
    for copy in rs_copies:
        copy.wait_send()
    for copy in ag_copies:
        copy.wait_send()
    for copy in back_copies:
        copy.wait()
    out_ref[...] = result[...]


def sum_over(partial, squares, n):
    v, cols = partial.shape
    half_cols = cols // 2
    per_row = min(n, half_cols // 128)
    width = half_cols // per_row
    rows = v // (n // per_row)
    dma = pltpu.SemaphoreType.DMA
    vm = pl.BlockSpec(memory_space=pltpu.VMEM)
    return pl.pallas_call(
        functools.partial(sum_kernel, n=n, rows=rows, width=width, per_row=per_row),
        in_specs=[vm, vm],
        out_specs=[vm, vm],
        out_shape=[jax.ShapeDtypeStruct((v, cols), F32), jax.ShapeDtypeStruct((8, 128), F32)],
        scratch_shapes=[
            pltpu.VMEM((v, half_cols), F32),
            pltpu.VMEM((v, half_cols), F32),
            pltpu.VMEM((n - 1, rows, width), F32),
            pltpu.VMEM((v, cols), F32),
            pltpu.VMEM((8, 128), F32),
            pltpu.VMEM((8, 128), F32),
            pltpu.VMEM((n, 8, 128), F32),
            pltpu.VMEM((rows, width), F32),
            dma((n,)), dma((n,)), dma((n - 1,)), dma((n - 1,)), dma((n - 1,)), dma((n - 1,)),
            dma((n,)), dma((n,)), dma((2,)), dma((n - 1,)), dma((n - 1,)),
        ],
        compiler_params=pltpu.CompilerParams(collective_id=0, has_side_effects=True),
        name="sum_over",
    )(partial, squares)


def from_both(x, half, axis):
    other = lax.ppermute(x, "paths", [(0, 1), (1, 0)])
    first = jnp.where(half == 0, x, other)
    second = jnp.where(half == 0, other, x)
    return jnp.concatenate([first, second], axis=axis)


def shards(total_features, chips, factors, frequency, phases, amplitude, targets, coeffs_init):
    half = lax.axis_index("paths")
    pick = half[None].astype(jnp.int32)
    v, block = coeffs_init.shape
    own_paths = targets.shape[1]
    mine = block // 2
    factors_all = from_both(factors, half, 0).astype(F32).astype(BF)
    targets_all = from_both(targets, half, 1)
    amp_row = amplitude[None, :]
    own_init = lax.dynamic_slice_in_dim(coeffs_init, half * mine, mine, 1)

    hi, lo, partial = build(pick, factors_all, frequency, phases[None, :], amp_row, coeffs_init, 256)
    predicted, _ = sum_over(partial, jnp.zeros((8, 128), F32), chips)
    coeffs = own_init
    velocity = jnp.zeros_like(own_init)
    tracked = jnp.zeros_like(predicted)
    for _ in range(ITERS):
        clipped = jnp.clip(predicted - targets_all, -huber_cap, huber_cap)
        gradient, push, squares = turn(pick, clipped, amp_row, hi, lo, 512)
        push, squares = sum_over(push, squares, chips)
        squares = squares[0, 0]
        scale = jnp.sqrt(squares / (v * total_features) + epsilon)
        velocity = momentum * velocity + gradient / scale
        coeffs = coeffs - step_rate * velocity
        tracked = momentum * tracked + push / scale
        predicted = predicted - step_rate * tracked
    coeffs = from_both(coeffs, half, 1)
    return coeffs, lax.dynamic_slice_in_dim(predicted, half * own_paths, own_paths, 1)


def solution(mesh):
    def body(factors, frequency, phases, amplitude, targets, coeffs_init):
        total = frequency.shape[1] * mesh.shape["feats"]
        return shards(total, mesh.shape["feats"], factors, frequency, phases, amplitude, targets, coeffs_init)

    return jax.shard_map(
        body,
        mesh=mesh,
        in_specs=(
            P(("groups", "paths"), None),
            P(None, "feats"),
            P("feats"),
            P("feats"),
            P(None, ("groups", "paths")),
            P(None, ("groups", "feats")),
        ),
        out_specs=(P(None, ("groups", "feats")), P(None, ("groups", "paths"))),
        check_vma=False,
    )
```

```python
import functools
import math

import jax
import jax.numpy as jnp
import numpy as np
from jax import lax
from jax.experimental import pallas as pl
from jax.experimental.pallas import tpu as pltpu
from jax.sharding import PartitionSpec as P

huber_cap = 1.0
step_rate = 0.2
momentum = 0.9
epsilon = 1e-06
ITERS = 3
BF = jnp.bfloat16
F32 = jnp.float32


def cosine_fit(degree):
    n = 64
    nodes = np.cos((np.arange(n) + 0.5) * np.pi / n)
    u = (nodes + 1.0) / 8.0
    cheb = np.polynomial.chebyshev.Chebyshev.fit(u, np.cos(2 * np.pi * np.sqrt(u)), degree, domain=[0.0, 0.25])
    return [float(c) for c in cheb.convert(kind=np.polynomial.Polynomial).coef]


COEFS = cosine_fit(5)
TURN = 0.0025 / (2.0 * math.pi)
MAGIC = 12582912.0


def cos_turns(t):
    k = (t + MAGIC) - MAGIC
    r = t - k
    u = r * r
    acc = u * COEFS[-1] + COEFS[-2]
    for c in COEFS[-3::-1]:
        acc = acc * u + c
    return acc


def split(x):
    hi = x.astype(BF)
    lo = (x - hi.astype(F32)).astype(BF)
    return hi, lo


def stacked(x):
    hi, lo = split(x)
    return jnp.concatenate([hi, lo], axis=0)


NT = (((1,), (1,)), ((), ()))


def build_kernel(half_ref, fac_ref, freq_ref, phase_ref, amp_ref, coef_ref, hi_ref, lo_ref, pred_ref, *, rows):
    @pl.when(pl.program_id(0) == 0)
    def _():
        pred_ref[...] = jnp.zeros_like(pred_ref)

    freq = freq_ref[...].astype(F32).astype(BF)
    phase = phase_ref[...].astype(F32) * (1.0 / 1024.0)
    chunks = fac_ref.shape[0] // rows
    v = coef_ref.shape[0]
    x = stacked(coef_ref[...] * amp_ref[...])

    def step(i, carry):
        at = pl.ds(pl.multiple_of(i * rows, rows), rows)
        summed = jnp.dot(fac_ref[at, :], freq, preferred_element_type=F32)
        c = cos_turns(summed * TURN + phase)
        hi, lo = split(c)
        hi_ref[at, :] = hi
        lo_ref[at, :] = lo
        out = lax.dot_general(x, hi, NT, preferred_element_type=F32)
        out = out + lax.dot_general(x, lo, NT, preferred_element_type=F32)
        pred_ref[:, at] += out[:v] + out[v:]
        return carry

    lax.fori_loop(0, chunks, step, 0, unroll=2)


def build(half, factors, frequency, phases, amplitude, coeffs, tile):
    paths, k = factors.shape
    v, whole = coeffs.shape
    mine = whole // 2
    nb = mine // tile
    at = lambda i, h: (0, h[0] * nb + i)
    return pl.pallas_call(
        functools.partial(build_kernel, rows=256),
        grid_spec=pltpu.PrefetchScalarGridSpec(
            num_scalar_prefetch=1,
            grid=(nb,),
            in_specs=[
                pl.BlockSpec((paths, k), lambda i, h: (0, 0)),
                pl.BlockSpec((k, tile), at),
                pl.BlockSpec((1, tile), at),
                pl.BlockSpec((1, tile), at),
                pl.BlockSpec((v, tile), at),
            ],
            out_specs=[
                pl.BlockSpec((paths, tile), lambda i, h: (0, i)),
                pl.BlockSpec((paths, tile), lambda i, h: (0, i)),
                pl.BlockSpec((v, paths), lambda i, h: (0, 0)),
            ],
        ),
        out_shape=[
            jax.ShapeDtypeStruct((paths, mine), BF),
            jax.ShapeDtypeStruct((paths, mine), BF),
            jax.ShapeDtypeStruct((v, paths), F32),
        ],
        name="build",
    )(half, factors, frequency, phases, amplitude, coeffs)


def turn_kernel(half_ref, clip_ref, amp_ref, hi_ref, lo_ref, grad_ref, push_ref, sq_ref, clip_pair):
    @pl.when(pl.program_id(0) == 0)
    def _():
        push_ref[...] = jnp.zeros_like(push_ref)
        sq_ref[...] = jnp.zeros_like(sq_ref)
        clip_pair[...] = stacked(clip_ref[...])

    v = grad_ref.shape[0]
    x = clip_pair[...]
    g = jnp.dot(x, hi_ref[...], preferred_element_type=F32)
    g = g + jnp.dot(x, lo_ref[...], preferred_element_type=F32)
    amp = amp_ref[...]
    grad = (g[:v] + g[v:]) * amp
    grad_ref[...] = grad
    square = grad * grad
    fold = sum(square[r : r + 8] for r in range(0, v, 8))
    sq_ref[...] += sum(fold[:, c : c + 128] for c in range(0, fold.shape[1], 128))
    y = stacked(grad * amp)
    out = lax.dot_general(y, hi_ref[...], NT, preferred_element_type=F32)
    out = out + lax.dot_general(y, lo_ref[...], NT, preferred_element_type=F32)
    push_ref[...] += out[:v] + out[v:]


def turn(half, clipped, amplitude, hi, lo, tile):
    v, paths = clipped.shape
    mine = hi.shape[1]
    nb = mine // tile
    return pl.pallas_call(
        turn_kernel,
        grid_spec=pltpu.PrefetchScalarGridSpec(
            num_scalar_prefetch=1,
            grid=(nb,),
            in_specs=[
                pl.BlockSpec((v, paths), lambda i, h: (0, 0)),
                pl.BlockSpec((1, tile), lambda i, h: (0, h[0] * nb + i)),
                pl.BlockSpec((paths, tile), lambda i, h: (0, i)),
                pl.BlockSpec((paths, tile), lambda i, h: (0, i)),
            ],
            out_specs=[
                pl.BlockSpec((v, tile), lambda i, h: (0, i)),
                pl.BlockSpec((v, paths), lambda i, h: (0, 0)),
                pl.BlockSpec((8, 128), lambda i, h: (0, 0)),
            ],
            scratch_shapes=[pltpu.VMEM((2 * v, paths), BF)],
        ),
        out_shape=[
            jax.ShapeDtypeStruct((v, mine), F32),
            jax.ShapeDtypeStruct((v, paths), F32),
            jax.ShapeDtypeStruct((8, 128), F32),
        ],
        name="turn",
    )(half, clipped, amplitude, hi, lo)


MESH = pl.DeviceIdType.MESH


def sum_kernel(*refs, n, rows, width, per_row, first, count):
    if first:
        x_ref, target_ref, pred_out, clip_out = refs[:4]
        refs = refs[4:]
    else:
        x_ref, sq_ref, grad_ref, pred_ref, track_ref, target_ref, pred_out, track_out, clip_out, sq_out, grad_out = refs[:11]
        grad_other, sq_pair, sq_mine, sq_all, sqp_sem, sqs_send, sqs_recv, grad_sem = refs[11:19]
        refs = refs[19:]
    from_pair, chip, pieces, result, total = refs[:5]
    pair_send, pair_recv, rs_send, rs_recv, ag_send, ag_recv, back_send, back_recv = refs[5:]
    v, half_cols = chip.shape
    core = lax.axis_index("paths")
    me = lax.axis_index("feats")
    other = 1 - core

    barrier = pltpu.get_barrier_semaphore()
    pl.semaphore_signal(barrier, inc=1, device_id={"paths": other}, device_id_type=MESH)
    for d in range(1, n):
        pl.semaphore_signal(barrier, inc=1, device_id={"feats": lax.rem(me + d, n)}, device_id_type=MESH)
    pl.semaphore_wait(barrier, n)

    def spot(j, base):
        r = pl.ds(pl.multiple_of((j // per_row) * rows, rows), rows)
        c = pl.ds(pl.multiple_of(base + lax.rem(j, per_row) * width, width), width)
        return r, c

    def to_pair(src, dst, ss, rs):
        return pltpu.make_async_remote_copy(src, dst, ss, rs, device_id={"paths": other}, device_id_type=MESH)

    def to_chip(src, dst, ss, rs, j):
        return pltpu.make_async_remote_copy(src, dst, ss, rs, device_id={"feats": j}, device_id_type=MESH)

    zero = 0
    if not first:
        sq_copy = to_pair(sq_ref, sq_pair, sqp_sem.at[0], sqp_sem.at[1])
        sq_copy.start()
    pair_copies = []
    for d in range(1, n + 1):
        j = lax.rem(me + d, n)
        r, c = spot(j, other * half_cols)
        r2, c2 = spot(j, zero)
        pair_copies.append(to_pair(x_ref.at[r, c], from_pair.at[r2, c2], pair_send.at[d - 1], pair_recv.at[d - 1]))
        pair_copies[-1].start()

    if not first:
        grad_copy = to_pair(grad_ref, grad_other, grad_sem.at[0], grad_sem.at[1])
        grad_copy.start()
        sq_copy.wait()
        sq_mine[...] = sq_ref[...] + sq_pair[...]
        sq_all[me] = sq_mine[...]
    rs_copies, sq_copies = [], []
    for d in range(1, n + 1):
        j = lax.rem(me + d, n)
        pair_copies[d - 1].wait_recv()
        r, c = spot(j, core * half_cols)
        r2, c2 = spot(j, zero)
        chip[r2, c2] = x_ref[r, c] + from_pair[r2, c2]
        if d < n:
            rs_copies.append(to_chip(chip.at[r2, c2], pieces.at[d - 1], rs_send.at[d - 1], rs_recv.at[d - 1], j))
            rs_copies[-1].start()
    for d in range(1, 1 if first else n):
        j = lax.rem(me + d, n)
        sq_copies.append(to_chip(sq_mine, sq_all.at[me], sqs_send.at[d - 1], sqs_recv.at[d - 1], j))
        sq_copies[-1].start()

    mr, mc = spot(me, zero)
    acc = chip[mr, mc]
    for d in range(1, n):
        rs_copies[d - 1].wait_recv()
        acc = acc + pieces[d - 1]
    total[...] = acc

    br, bc = spot(me, core * half_cols)
    ag_copies, back_copies = [], []
    for d in range(1, n):
        j = lax.rem(me + d, n)
        ag_copies.append(to_chip(total, result.at[br, bc], ag_send.at[d - 1], ag_recv.at[d - 1], j))
        ag_copies[-1].start()
    back_copies.append(to_pair(total, result.at[br, bc], back_send.at[0], back_recv.at[0]))
    back_copies[0].start()
    result[br, bc] = acc
    for d in range(1, n):
        ag_copies[d - 1].wait_recv()
        source = lax.rem(me + n - d, n)
        r, c = spot(source, core * half_cols)
        back_copies.append(to_pair(result.at[r, c], result.at[r, c], back_send.at[d], back_recv.at[d]))
        back_copies[-1].start()
    if not first:
        grad_copy.wait()
        grad_out[...] = grad_other[...]
    for copy in sq_copies:
        copy.wait()
    for copy in pair_copies:
        copy.wait_send()
    for copy in rs_copies:
        copy.wait_send()
    for copy in ag_copies:
        copy.wait_send()
    for copy in back_copies:
        copy.wait()
    if first:
        predicted = result[...]
    else:
        squares = jnp.sum(sq_all[...], axis=0)
        squares = jnp.sum(jnp.sum(squares, axis=0, keepdims=True), axis=1, keepdims=True)
        scale = jnp.sqrt(squares / count + epsilon)
        sq_out[...] = jnp.broadcast_to(scale, sq_out.shape)
        tracked = momentum * track_ref[...] + result[...] / scale
        track_out[...] = tracked
        predicted = pred_ref[...] - step_rate * tracked
    pred_out[...] = predicted
    clip_out[...] = jnp.clip(predicted - target_ref[...], -huber_cap, huber_cap)


def sum_over(operands, n, count):
    v, cols = operands[0].shape
    first = len(operands) == 2
    half_cols = cols // 2
    per_row = min(n, half_cols // 128)
    width = half_cols // per_row
    rows = v // (n // per_row)
    dma = pltpu.SemaphoreType.DMA
    vm = pl.BlockSpec(memory_space=pltpu.VMEM)
    image = jax.ShapeDtypeStruct((v, cols), F32)
    outs = [image, image]
    extra = []
    if not first:
        grad = operands[2].shape
        outs = [image, image, image, jax.ShapeDtypeStruct((8, 128), F32), jax.ShapeDtypeStruct(grad, F32)]
        extra = [
            pltpu.VMEM(grad, F32),
            pltpu.VMEM((8, 128), F32),
            pltpu.VMEM((8, 128), F32),
            pltpu.VMEM((n, 8, 128), F32),
            dma((2,)),
            dma((n - 1,)),
            dma((n - 1,)),
            dma((2,)),
        ]
    return pl.pallas_call(
        functools.partial(sum_kernel, n=n, rows=rows, width=width, per_row=per_row, first=first, count=count),
        in_specs=[vm] * len(operands),
        out_specs=[vm] * len(outs),
        out_shape=outs,
        scratch_shapes=extra
        + [
            pltpu.VMEM((v, half_cols), F32),
            pltpu.VMEM((v, half_cols), F32),
            pltpu.VMEM((n - 1, rows, width), F32),
            pltpu.VMEM((v, cols), F32),
            pltpu.VMEM((rows, width), F32),
            dma((n,)), dma((n,)), dma((n - 1,)), dma((n - 1,)), dma((n - 1,)), dma((n - 1,)), dma((n,)), dma((n,)),
        ],
        compiler_params=pltpu.CompilerParams(collective_id=0 if first else 1, has_side_effects=True),
        name="sum_first" if first else "sum_over",
    )(*operands)


def finish_kernel(*refs, iters):
    init_ref, pred_ref = refs[:2]
    mine, other, scales = refs[2 : 2 + iters], refs[2 + iters : 2 + 2 * iters], refs[2 + 2 * iters : 2 + 3 * iters]
    coef_out, pred_out = refs[2 + 3 * iters :]
    half = lax.axis_index("paths")
    width = mine[0].shape[1]
    own = pred_out.shape[1]
    for grads, where in ((mine, half), (other, 1 - half)):
        at = pl.ds(pl.multiple_of(where * width, width), width)
        coeffs = init_ref[:, at]
        velocity = jnp.zeros_like(coeffs)
        for g, s in zip(grads, scales):
            velocity = momentum * velocity + g[...] / s[0:1, 0:1]
            coeffs = coeffs - step_rate * velocity
        coef_out[:, at] = coeffs
    pred_out[...] = pred_ref[:, pl.ds(pl.multiple_of(half * own, own), own)]


def finish(init, predicted, mine, other, scales, own_paths):
    v = init.shape[0]
    vm = pl.BlockSpec(memory_space=pltpu.VMEM)
    return pl.pallas_call(
        functools.partial(finish_kernel, iters=len(mine)),
        in_specs=[vm] * (2 + 3 * len(mine)),
        out_specs=[vm, vm],
        out_shape=[jax.ShapeDtypeStruct(init.shape, F32), jax.ShapeDtypeStruct((v, own_paths), F32)],
        name="finish",
    )(init, predicted, *mine, *other, *scales)


def from_both(x, half, axis):
    other = lax.ppermute(x, "paths", [(0, 1), (1, 0)])
    first = jnp.where(half == 0, x, other)
    second = jnp.where(half == 0, other, x)
    return jnp.concatenate([first, second], axis=axis)


def shards(total_features, chips, factors, frequency, phases, amplitude, targets, coeffs_init):
    half = lax.axis_index("paths")
    pick = half[None].astype(jnp.int32)
    v = coeffs_init.shape[0]
    own_paths = targets.shape[1]
    factors_all = from_both(factors, half, 0).astype(F32).astype(BF)
    targets_all = from_both(targets, half, 1)
    amp_row = amplitude[None, :]

    hi, lo, partial = build(pick, factors_all, frequency, phases[None, :], amp_row, coeffs_init, 256)
    predicted, clipped = sum_over((partial, targets_all), chips, None)
    tracked = jnp.zeros_like(predicted)
    mine, other, scales = [], [], []
    for _ in range(ITERS):
        gradient, push, squares = turn(pick, clipped, amp_row, hi, lo, 512)
        state = (push, squares, gradient, predicted, tracked, targets_all)
        predicted, tracked, clipped, scale, partner = sum_over(state, chips, float(v * total_features))
        mine.append(gradient)
        other.append(partner)
        scales.append(scale)
    return finish(coeffs_init, predicted, mine, other, scales, own_paths)


def solution(mesh):
    def body(factors, frequency, phases, amplitude, targets, coeffs_init):
        total = frequency.shape[1] * mesh.shape["feats"]
        return shards(total, mesh.shape["feats"], factors, frequency, phases, amplitude, targets, coeffs_init)

    return jax.shard_map(
        body,
        mesh=mesh,
        in_specs=(
            P(("groups", "paths"), None),
            P(None, "feats"),
            P("feats"),
            P("feats"),
            P(None, ("groups", "paths")),
            P(None, ("groups", "feats")),
        ),
        out_specs=(P(None, ("groups", "feats")), P(None, ("groups", "paths"))),
        check_vma=False,
    )
```
